256 devices in a mesh: gx: 8 (over x, core), gy: 4 (over y), gz: 8 (over z).
Axes of the slice: x: 4, y: 4, z: 8, core: 2. Of those that a mesh axis runs over, the one named last changes fastest.
Arguments:
- facies: int32 [128, 128, 512], P('gz', 'gx', 'gy'), may hold values from 0 to 15
- perm_table: float32 [3, 16], replicated, may hold values from 0.0003 to 3, as said below
- line_breaks: int32 [127], replicated, may hold values 0 or 1
Outputs:
- pressure: float32 [3, 128, 128, 512], P(None, 'gz', 'gx', 'gy')
- residual: float32 [3, 128, 128, 512], P(None, 'gz', 'gx', 'gy')
The draws below stay inside these ranges and needn't reach their ends.
Inputs may be any that keep to these rules, and one draw needn't show every extreme that they name: `perm_table`: positive coefficients.
All inputs are finite; a program needn't handle non-finite values.
Results may differ from the reference program's by a relative error of at most 0.0003.
Values sent between devices are 32-bit elements; how exact they have to be, the bound alone decides.
A program may use at most 64 MiB of HBM per device.

```python
import math
import jax
import jax.numpy as jnp
from jax import lax

NF = 16
NX = 128
NY = 512
NZ = 128


def draw_perm_table(key, part):
    spread = jax.random.uniform(key, (3, NF), jnp.float32)
    floor = jnp.array([[0.0003], [0.0003], [0.3]], jnp.float32)
    return floor * jnp.exp(spread * math.log(10.0))


def place_ends(values, key, smallest, high):
    longest = values.shape.index(max(values.shape))
    spots = []
    for shift in (0, 1):
        where = [jax.random.randint(jax.random.fold_in(key, axis), (), 0, length) for axis, length in enumerate(values.shape)]
        where[longest] = (where[longest] + shift) % values.shape[longest]
        spots.append(tuple(where))
    return values.at[spots[0]].set(smallest).at[spots[1]].set(high)


def setup_inputs(seed: int = 0) -> dict:
    streams_of = jax.random.split(jax.random.key(seed), 4)
    return {
        "facies": place_ends(jax.random.randint(streams_of[0], (NZ, NX, NY), 0, NF), jax.random.fold_in(streams_of[0], 1), 0, NF - 1).astype(jnp.int32),
        "perm_table": draw_perm_table(jax.random.fold_in(streams_of[3], 71), 0),
        "line_breaks": place_ends((jax.random.randint(streams_of[2], (NZ - 1,), 0, 16) < 1).astype(jnp.int32), jax.random.fold_in(streams_of[2], 1), 0, 1),
    }


def six_sides(padded):
    return (padded[..., :-2, 1:-1, 1:-1], padded[..., 2:, 1:-1, 1:-1],
            padded[..., 1:-1, :-2, 1:-1], padded[..., 1:-1, 2:, 1:-1],
            padded[..., 1:-1, 1:-1, :-2], padded[..., 1:-1, 1:-1, 2:])


def face_pair(centre, beside):
    inside = beside > 0.0
    harmonic = 2.0 * centre * beside / (centre + beside)
    return (jnp.where(inside, harmonic, 2.0 * centre), jnp.where(inside, harmonic, centre),
            jnp.where(inside, harmonic, 0.0))


def assemble(perm, padded):
    z_sides = six_sides(padded[2])
    x_sides = six_sides(padded[0])
    y_sides = six_sides(padded[1])
    z_low = face_pair(perm[2], z_sides[0])
    z_high = face_pair(perm[2], z_sides[1])
    x_low = face_pair(perm[0], x_sides[2])
    x_high = face_pair(perm[0], x_sides[3])
    y_low = face_pair(perm[1], y_sides[4])
    y_high = face_pair(perm[1], y_sides[5])
    taus = (z_low[0], z_high[0], x_low[0], x_high[0], y_low[0], y_high[0])
    source = jnp.stack([x_high[1] - x_low[1], y_high[1] - y_low[1], z_high[1] - z_low[1]])
    centre_sum = taus[0] + taus[1] + taus[2] + taus[3] + taus[4] + taus[5]
    return taus, source, centre_sum, z_low[2], z_high[2]


def explicit_terms(taus, sides, break_low, break_high):
    return (taus[2] * sides[2] + taus[3] * sides[3] + taus[4] * sides[4] + taus[5] * sides[5]
            + taus[0] * break_low * sides[0] + taus[1] * break_high * sides[1])


def residual_of(taus, sides, source, centre_sum, field):
    total = (taus[0] * sides[0] + taus[1] * sides[1] + taus[2] * sides[2]
             + taus[3] * sides[3] + taus[4] * sides[4] + taus[5] * sides[5])
    return source - centre_sum * field + total


def line_solve(sub_diag, main_diag, super_diag, right):
    columns = jnp.moveaxis(right, 1, 0)

    def forward(carry, item):
        ratio_prior, value_prior = carry
        below, centre, above, value = item
        pivot = centre - below * ratio_prior
        ratio = above / pivot
        current = (value - below[None] * value_prior) / pivot[None]
        return (ratio, current), (ratio, current)

    start = (jnp.zeros(main_diag.shape[1:], jnp.float32), jnp.zeros(columns.shape[1:], jnp.float32))
    _, (ratios, partial_value) = lax.scan(forward, start, (sub_diag, main_diag, super_diag, columns))

    def backward(later, item):
        ratio, value = item
        current = value - ratio[None] * later
        return current, current

    _, result = lax.scan(backward, jnp.zeros(columns.shape[1:], jnp.float32), (ratios, partial_value), reverse=True)
    return jnp.moveaxis(result, 0, 1)


def reference(facies, perm_table, line_breaks):
    perm = perm_table[:, facies]
    widths = ((0, 0), (1, 1), (1, 1), (1, 1))
    taus, source, centre_sum, link_low, link_high = assemble(perm, jnp.pad(perm, widths))
    extended = jnp.concatenate([jnp.zeros((1,), jnp.int32), line_breaks, jnp.zeros((1,), jnp.int32)]).astype(jnp.float32)
    break_low = extended[:NZ][:, None, None]
    break_high = extended[1:][:, None, None]
    sub_diag = -link_low * (1.0 - break_low)
    super_diag = -link_high * (1.0 - break_high)
    first = line_solve(sub_diag, centre_sum, super_diag, source)
    right = source + explicit_terms(taus, six_sides(jnp.pad(first, widths)), break_low, break_high)
    second = line_solve(sub_diag, centre_sum, super_diag, right)
    residual = residual_of(taus, six_sides(jnp.pad(second, widths)), source, centre_sum, second)
    return second, residual
```

```python
import jax
import jax.numpy as jnp
from jax import lax
from jax.sharding import PartitionSpec as P


def from_prev(block, axis):
    size = lax.axis_size(axis)
    return lax.ppermute(block, axis, [(i, i + 1) for i in range(size - 1)])


def from_next(block, axis):
    size = lax.axis_size(axis)
    return lax.ppermute(block, axis, [(i + 1, i) for i in range(size - 1)])


def neighbours(values, axis, dim):
    n = values.shape[dim]
    low = from_prev(lax.slice_in_dim(values, n - 1, n, axis=dim), axis)
    high = from_next(lax.slice_in_dim(values, 0, 1, axis=dim), axis)
    below = jnp.concatenate([low, lax.slice_in_dim(values, 0, n - 1, axis=dim)], dim)
    above = jnp.concatenate([lax.slice_in_dim(values, 1, n, axis=dim), high], dim)
    return below, above


def shifted(values, low, high, dim):
    n = values.shape[dim]
    below = jnp.concatenate([low, lax.slice_in_dim(values, 0, n - 1, axis=dim)], dim)
    above = jnp.concatenate([lax.slice_in_dim(values, 1, n, axis=dim), high], dim)
    return below, above


def face_pair(centre, beside):
    inside = beside > 0.0
    harmonic = 2.0 * centre * beside / (centre + beside)
    return (
        jnp.where(inside, harmonic, 2.0 * centre),
        jnp.where(inside, harmonic, centre),
        jnp.where(inside, harmonic, 0.0),
    )


def table_lookup(facies, perm_table):
    perm = jnp.zeros((3,) + facies.shape, jnp.float32)
    for label in range(perm_table.shape[1]):
        perm = jnp.where((facies == label)[None], perm_table[:, label][:, None, None, None], perm)
    return perm


def shift_rows(values, stride, fill, axis):
    count = values.shape[axis]
    step = abs(stride)
    filler = jnp.full_like(lax.slice_in_dim(values, 0, step, axis=axis), fill)
    if stride > 0:
        return jnp.concatenate([filler, lax.slice_in_dim(values, 0, count - step, axis=axis)], axis)
    return jnp.concatenate([lax.slice_in_dim(values, step, count, axis=axis), filler], axis)


def interior_solve(sub_diag, main_diag, super_diag, columns):
    stride = 1
    count = main_diag.shape[0]
    while stride < count:
        sub_low = shift_rows(sub_diag, stride, 0.0, 0)
        super_low = shift_rows(super_diag, stride, 0.0, 0)
        main_low = shift_rows(main_diag, stride, 1.0, 0)
        column_low = shift_rows(columns, stride, 0.0, 1)
        sub_high = shift_rows(sub_diag, -stride, 0.0, 0)
        super_high = shift_rows(super_diag, -stride, 0.0, 0)
        main_high = shift_rows(main_diag, -stride, 1.0, 0)
        column_high = shift_rows(columns, -stride, 0.0, 1)
        left = sub_diag / main_low
        right = super_diag / main_high
        main_diag = main_diag - left * super_low - right * sub_high
        columns = columns - left[None] * column_low - right[None] * column_high
        sub_diag = -left * sub_low
        super_diag = -right * super_high
        stride *= 2
    return columns / main_diag[None]


def lateral_sides(field):
    x_low, x_high = neighbours(field, "gx", 2)
    y_low, y_high = neighbours(field, "gy", 3)
    return x_low, x_high, y_low, y_high


def per_device(facies, perm_table, line_breaks):
    depth = facies.shape[0]
    inner = depth - 2
    count = lax.axis_size("gz")
    position = lax.axis_index("gz")
    perm = table_lookup(facies, perm_table)
    px, py, pz = perm[0], perm[1], perm[2]
    z_below, z_above = neighbours(pz, "gz", 0)
    x_below, x_above = neighbours(px, "gx", 1)
    y_below, y_above = neighbours(py, "gy", 2)
    z_low = face_pair(pz, z_below)
    z_high = face_pair(pz, z_above)
    x_low = face_pair(px, x_below)
    x_high = face_pair(px, x_above)
    y_low = face_pair(py, y_below)
    y_high = face_pair(py, y_above)
    taus = (z_low[0], z_high[0], x_low[0], x_high[0], y_low[0], y_high[0])
    source = jnp.stack([x_high[1] - x_low[1], y_high[1] - y_low[1], z_high[1] - z_low[1]])
    centre_sum = taus[0] + taus[1] + taus[2] + taus[3] + taus[4] + taus[5]
    link_low, link_high = z_low[2], z_high[2]

    extended = jnp.concatenate(
        [jnp.zeros((1,), jnp.int32), line_breaks, jnp.zeros((1,), jnp.int32)]
    ).astype(jnp.float32)
    window = lax.dynamic_slice_in_dim(extended, position * depth, depth + 1)
    break_low = window[:depth][:, None, None]
    break_high = window[1:][:, None, None]
    sub_diag = -link_low * (1.0 - break_low)
    super_diag = -link_high * (1.0 - break_high)
    single_row = jnp.zeros_like(sub_diag[1:2])
    blank = jnp.zeros((inner - 1,) + sub_diag.shape[1:], jnp.float32)
    inner_sub = jnp.concatenate([single_row, sub_diag[2 : depth - 1]])
    inner_super = jnp.concatenate([super_diag[1 : depth - 2], single_row])
    inner_main = centre_sum[1 : depth - 1]
    push_low = jnp.concatenate([-sub_diag[1:2], blank])
    push_high = jnp.concatenate([blank, -super_diag[depth - 2 : depth - 1]])
    columns = jnp.concatenate([source[:, 1 : depth - 1], push_low[None], push_high[None]])
    solved = interior_solve(inner_sub, inner_main, inner_super, columns)
    inner_first = solved[:3]
    weight_low = solved[3]
    weight_high = solved[4]
    lower_u = sub_diag[0]
    centre_u = centre_sum[0] + super_diag[0] * weight_low[0]
    upper_u = super_diag[0] * weight_high[0]
    lower_v = sub_diag[depth - 1] * weight_low[inner - 1]
    centre_v = centre_sum[depth - 1] + sub_diag[depth - 1] * weight_high[inner - 1]
    upper_v = super_diag[depth - 1]

    def reduced_source(right, interior):
        return jnp.stack(
            [
                right[:, 0] - super_diag[0][None] * interior[:, 0],
                right[:, depth - 1] - sub_diag[depth - 1][None] * interior[:, inner - 1],
            ]
        )

    def rebuild(interior, ends):
        middle = (
            interior + weight_low[None] * ends[0][:, None] + weight_high[None] * ends[1][:, None]
        )
        return jnp.concatenate([ends[0][:, None], middle, ends[1][:, None]], axis=1)

    coefficients = jnp.stack([lower_u, centre_u, upper_u, lower_v, centre_v, upper_v])
    pair_first = reduced_source(source, inner_first)
    packed = jnp.concatenate([coefficients, pair_first.reshape((6,) + lower_u.shape)])
    gathered = lax.all_gather(packed, "gz")
    lower, diag, upper = [], [], []
    for k in range(count):
        lower += [gathered[k, 0], gathered[k, 3]]
        diag += [gathered[k, 1], gathered[k, 4]]
        upper += [gathered[k, 2], gathered[k, 5]]
    unknowns = 2 * count
    pivots, ratios = [], []
    for i in range(unknowns):
        pivot = diag[i] if i == 0 else diag[i] - lower[i] * ratios[i - 1]
        pivots.append(pivot)
        ratios.append(upper[i] / pivot)

    def reduced_solve(rhs):
        partial = []
        for i in range(unknowns):
            value = rhs[i] if i == 0 else rhs[i] - lower[i][None] * partial[i - 1]
            partial.append(value / pivots[i][None])
        result = [None] * unknowns
        result[unknowns - 1] = partial[unknowns - 1]
        for i in range(unknowns - 2, -1, -1):
            result[i] = partial[i] - ratios[i][None] * result[i + 1]
        zero = jnp.zeros_like(result[0])
        padded = jnp.stack([zero] + result + [zero])
        return lax.dynamic_slice_in_dim(padded, 2 * position, 4)

    def rhs_list(pairs):
        values = []
        for k in range(count):
            values += [pairs[k, 0], pairs[k, 1]]
        return values

    ends_first = reduced_solve(rhs_list(gathered[:, 6:].reshape((count, 2, 3) + lower_u.shape)))
    first = rebuild(inner_first, ends_first[1:3])
    f_z_low, f_z_high = shifted(first, ends_first[0][:, None], ends_first[3][:, None], 1)
    f_x_low, f_x_high, f_y_low, f_y_high = lateral_sides(first)
    right = source + (
        taus[2] * f_x_low
        + taus[3] * f_x_high
        + taus[4] * f_y_low
        + taus[5] * f_y_high
        + taus[0] * break_low * f_z_low
        + taus[1] * break_high * f_z_high
    )
    inner_second = interior_solve(inner_sub, inner_main, inner_super, right[:, 1 : depth - 1])
    pair_second = reduced_source(right, inner_second)
    gathered_second = lax.all_gather(pair_second, "gz")
    ends_second = reduced_solve(rhs_list(gathered_second))
    second = rebuild(inner_second, ends_second[1:3])
    s_z_low, s_z_high = shifted(second, ends_second[0][:, None], ends_second[3][:, None], 1)
    s_x_low, s_x_high, s_y_low, s_y_high = lateral_sides(second)
    total = (
        taus[0] * s_z_low
        + taus[1] * s_z_high
        + taus[2] * s_x_low
        + taus[3] * s_x_high
        + taus[4] * s_y_low
        + taus[5] * s_y_high
    )
    residual = source - centre_sum * second + total
    return (second, residual)


def solution(mesh):
    return jax.shard_map(
        per_device,
        mesh=mesh,
        in_specs=(P("gz", "gx", "gy"), P(), P()),
        out_specs=(P(None, "gz", "gx", "gy"), P(None, "gz", "gx", "gy")),
        check_vma=False,
    )
```
